32 devices in a mesh: dp: 8 (over z, x), seq: 4 (over y, core).
Axes of the slice: x: 2, y: 2, z: 4, core: 2. Of those that a mesh axis runs over, the one named last changes fastest.
Arguments:
- block_input: float32 [4096, 2048], P(('dp', 'seq')), may hold values from -6 to 6
- segments: int32 [8, 512], P('dp', 'seq'), may hold values from 0 to 3, never falling along the last dimension, each value on 1 to 256 neighbouring positions
- cotangent: float32 [4096, 2048], P(('dp', 'seq')), may hold values from -6 to 6
- gain_attn: bfloat16 [2048], P(('dp', 'seq')), may hold values from 0.5 to 1.5
- w_query: bfloat16 [2048, 1024], P(('dp', 'seq')), may hold values from -0.125 to 0.125
- w_key: bfloat16 [2048, 1024], P(('dp', 'seq')), may hold values from -0.125 to 0.125
- w_value: bfloat16 [2048, 1728], P(('dp', 'seq')), may hold values from -0.125 to 0.125
- w_gate: bfloat16 [2048, 1728], P(('dp', 'seq')), may hold values from -0.125 to 0.125
- w_out: bfloat16 [1728, 2048], P(None, ('dp', 'seq')), may hold values from -0.15625 to 0.15625
- gain_mlp: bfloat16 [2048], P(('dp', 'seq')), may hold values from 0.5 to 1.5
- w_up: bfloat16 [2048, 1728], P(('dp', 'seq')), may hold values from -0.125 to 0.125
- w_act: bfloat16 [2048, 1728], P(('dp', 'seq')), may hold values from -0.125 to 0.125
- w_down: bfloat16 [1728, 2048], P(None, ('dp', 'seq')), may hold values from -0.15625 to 0.15625
Outputs:
- block_out: float32 [4096, 2048], P(('dp', 'seq'))
- grad_input: float32 [4096, 2048], P(('dp', 'seq'))
- grad_gain_attn: float32 [2048], P(('dp', 'seq'))
- grad_query: float32 [2048, 1024], P(('dp', 'seq'))
- grad_key: float32 [2048, 1024], P(('dp', 'seq'))
- grad_value: float32 [2048, 1728], P(('dp', 'seq'))
- grad_gate: float32 [2048, 1728], P(('dp', 'seq'))
- grad_out: float32 [1728, 2048], P(None, ('dp', 'seq'))
- grad_gain_mlp: float32 [2048], P(('dp', 'seq'))
- grad_up: float32 [2048, 1728], P(('dp', 'seq'))
- grad_act: float32 [2048, 1728], P(('dp', 'seq'))
- grad_down: float32 [1728, 2048], P(None, ('dp', 'seq'))
The draws below stay inside these ranges and needn't reach their ends.
All inputs are finite; a program needn't handle non-finite values.
Results may differ from the reference program's by a relative error of at most 0.0098.
Values may be sent and summed in bfloat16 or wider, within the bound.
No kernel may reach another device: no remote copies, remote signals or barrier semaphores. Data moves between devices by JAX's collectives and lax.ppermute only.
A program may use at most 320 MiB of HBM per device.

```python
import math
import jax
import jax.numpy as jnp
import numpy as np
from jax import lax

D = 2048
H = 4
DK = 256
DV = 432
FF = 1728
NSEG = 4
QK = 1024
VW = 1728
SEQ = 512
SEG_MOST = 256
NSEQ = 8
TOKENS = 4096


def block_levels(rng, dims, pieces, low, top_value):
    factor_of, own = 1.0, jax.random.fold_in(rng, 6)
    for dim, shards_of in pieces:
        heights = jnp.exp(jax.random.uniform(jax.random.fold_in(own, dim), (shards_of,), jnp.float32, low / len(pieces), top_value / len(pieces)))
        factor_of = factor_of * jnp.repeat(heights, dims[dim] // shards_of).reshape([-1 if axis == dim else 1 for axis in range(len(dims))])
    return factor_of


def split_up(count, total, reach, slope):
    loads = [(1 << 20) // math.isqrt(grade ** slope) + 1 for grade in range(2, count + 1)]
    rest, counts = total - reach - (count - 1), [1] * (count - 1)
    while rest > 0:
        movable = [i for i in range(count - 1) if counts[i] < reach]
        whole, budget = sum([loads[i] for i in movable]), rest
        for i in movable:
            extra = min(reach - counts[i], max(1, budget * loads[i] // whole), rest)
            counts[i] = counts[i] + extra
            rest = rest - extra
    return np.array([reach] + counts)


def ragged_sizes(stream_key, amount, total, bound, slope):
    if amount == 2:
        one = jax.random.randint(stream_key, (), max(1, total - bound), min(bound, total - 1) + 1)
        return jnp.stack([one, total - one])
    tallies = jnp.asarray(split_up(amount, total, bound, slope), jnp.int32)
    twos = (amount - 1) // 2
    source_of, receiver = tallies[1:1 + 2 * twos:2], tallies[2:2 + 2 * twos:2]
    margin = jnp.minimum(source_of - 1, bound - receiver)
    passed = jax.random.randint(jax.random.fold_in(stream_key, 1), (twos,), 0, 1 << 20) % (margin + 1)
    tallies = tallies.at[1:1 + 2 * twos:2].set(source_of - passed).at[2:2 + 2 * twos:2].set(receiver + passed)
    return tallies[jax.random.permutation(jax.random.fold_in(stream_key, 2), amount)]


def gaussian(rng, shape, deviation, reach, cuts=(), held_as=jnp.bfloat16):
    loudness = block_levels(rng, shape, cuts, -0.22, 0.18) if cuts else 1.0
    array = jax.random.normal(rng, shape, jnp.float32) * deviation * loudness
    return jnp.minimum(jnp.maximum(array, -reach), reach).astype(held_as)


def setup_inputs(seed: int = 0) -> dict:
    seeds = jax.random.split(jax.random.key(seed), 14)
    block_input = gaussian(seeds[0], (TOKENS, D), 1.0, 6.0, ((0, 32),), jnp.float32)
    segments = jax.vmap(lambda own: jnp.searchsorted(jnp.cumsum(ragged_sizes(own, NSEG, SEQ, SEG_MOST, 0)), jnp.arange(SEQ), side="right"))(jax.random.split(seeds[1], NSEQ)).reshape((NSEQ, SEQ)).astype(jnp.int32)
    cotangent = gaussian(seeds[2], (TOKENS, D), 1.0, 6.0, ((0, 32),), jnp.float32)
    gain_attn = jnp.clip(1.0 + 0.1 * jax.random.normal(seeds[3], (D,), jnp.float32), 0.5, 1.5).astype(jnp.bfloat16)
    w_query = gaussian(seeds[4], (D, QK), D ** -0.5, 0.125, ((0, 32),))
    w_key = gaussian(seeds[5], (D, QK), D ** -0.5, 0.125, ((0, 32),))
    w_value = gaussian(seeds[6], (D, VW), D ** -0.5, 0.125, ((0, 32),))
    w_gate = gaussian(seeds[7], (D, VW), D ** -0.5, 0.125, ((0, 32),))
    w_out = gaussian(seeds[8], (VW, D), VW ** -0.5, 0.15625, ((1, 32),))
    gain_mlp = jnp.clip(1.0 + 0.1 * jax.random.normal(seeds[9], (D,), jnp.float32), 0.5, 1.5).astype(jnp.bfloat16)
    w_up = gaussian(seeds[10], (D, FF), D ** -0.5, 0.125, ((0, 32),))
    w_act = gaussian(seeds[11], (D, FF), D ** -0.5, 0.125, ((0, 32),))
    w_down = gaussian(seeds[12], (FF, D), FF ** -0.5, 0.15625, ((1, 32),))
    return {"block_input": block_input, "segments": segments, "cotangent": cotangent, "gain_attn": gain_attn, "w_query": w_query, "w_key": w_key, "w_value": w_value, "w_gate": w_gate, "w_out": w_out, "gain_mlp": gain_mlp, "w_up": w_up, "w_act": w_act, "w_down": w_down}


EPS = 1e-06
HEAD_FLOOR = 1.0
HIGH = lax.Precision.HIGHEST
SQRT_HALF = 0.7071067811865476
INV_ROOT_TWO_PI = 0.3989422804014327

def log_decay(count):
    return jnp.log1p(-jnp.exp2(-5.0 - jnp.arange(count, dtype=jnp.float32)))

def times(left, right):
    return jnp.dot(left, right, preferred_element_type=jnp.float32)

def left_contract(left, right):
    return lax.dot_general(left, right, (((0,), (0,)), ((), ())), preferred_element_type=jnp.float32)

def right_contract(left, right):
    return lax.dot_general(left, right, (((1,), (1,)), ((), ())), preferred_element_type=jnp.float32)

def rms_forward(value, gain):
    scale = lax.rsqrt(lax.optimization_barrier(jnp.mean(value * value, axis=-1, keepdims=True)) + EPS)
    normed = value * scale
    return (normed, scale, (normed * gain.astype(jnp.float32)).astype(jnp.bfloat16))

def rms_backward(d_act, normed, scale, gain):
    d_gain = lax.optimization_barrier(jnp.sum(d_act * normed, axis=0))
    d_norm = d_act * gain.astype(jnp.float32)
    d_in = scale * (d_norm - normed * lax.optimization_barrier(jnp.mean(d_norm * normed, axis=-1, keepdims=True)))
    return (d_in, d_gain)

def head_forward(value):
    scale = lax.rsqrt(lax.optimization_barrier(jnp.mean(value * value, axis=-1, keepdims=True)) + HEAD_FLOOR)
    return (value * scale, scale)

def head_backward(d_normed, normed, scale):
    return scale * (d_normed - normed * lax.optimization_barrier(jnp.mean(d_normed * normed, axis=-1, keepdims=True)))

def swish_parts(value):
    sig = jax.nn.sigmoid(value)
    return (value * sig, sig * (1.0 + value * (1.0 - sig)))

def gelu_parts(value):
    cdf = 0.5 * (1.0 + lax.erf(value * SQRT_HALF))
    dens = jnp.exp(-0.5 * value * value) * INV_ROOT_TWO_PI
    return (value * cdf, cdf + value * dens)

def retention_full(query, keys, values, seg):
    length = query.shape[0]
    pos = jnp.arange(length, dtype=jnp.float32)
    diff = pos[:, None] - pos[None, :]
    allowed = (diff >= 0) & (seg[:, None] == seg[None, :])
    decay = jnp.exp(jnp.maximum(diff, 0.0)[None] * log_decay(query.shape[1])[:, None, None])
    mask = jnp.where(allowed[None], decay, 0.0)
    scores = jnp.einsum('thd,shd->hts', query, keys, precision=HIGH) * mask
    return jnp.einsum('hts,she->the', scores, values, precision=HIGH)

def sequence_step(params, tokens, seg, cot):
    gain_first, query_full, key_full, value_full, gate_full, out_full, gain_second, up_full, act_full, down_full = params
    length = tokens.shape[0]
    norm_one, rms_one, act_one = rms_forward(tokens, gain_first)
    query = times(act_one, query_full).reshape(length, H, DK)
    keys = (times(act_one, key_full) * DK ** (-0.5)).reshape(length, H, DK)
    values = times(act_one, value_full).reshape(length, H, DV)
    zgate = times(act_one, gate_full)
    ret = retention_full(query, keys, values, seg)
    retn, hscale = head_forward(ret)
    swish_val, swish_slope = swish_parts(zgate)
    retn_flat = retn.reshape(length, VW)
    mixed = (swish_val * retn_flat).astype(jnp.bfloat16)
    resid = tokens + times(mixed, out_full)
    norm_two, rms_two, act_two = rms_forward(resid, gain_second)
    upper = times(act_two, up_full)
    pregate = times(act_two, act_full)
    gelu_val, gelu_slope = gelu_parts(pregate)
    hidden = (gelu_val * upper).astype(jnp.bfloat16)
    block_out = resid + times(hidden, down_full)
    cot_half = cot.astype(jnp.bfloat16)
    grad_down = left_contract(hidden, cot_half)
    d_hidden = right_contract(cot_half, down_full)
    d_pre = (d_hidden * upper * gelu_slope).astype(jnp.bfloat16)
    d_upper = (d_hidden * gelu_val).astype(jnp.bfloat16)
    grad_up = left_contract(act_two, d_upper)
    grad_act = left_contract(act_two, d_pre)
    d_act_two = right_contract(d_upper, up_full) + right_contract(d_pre, act_full)
    d_norm_two, grad_gain_mlp = rms_backward(d_act_two, norm_two, rms_two, gain_second)
    d_resid = cot + d_norm_two
    resid_half = d_resid.astype(jnp.bfloat16)
    grad_out = left_contract(mixed, resid_half)
    d_mixed = right_contract(resid_half, out_full)
    d_zgate = (d_mixed * retn_flat * swish_slope).astype(jnp.bfloat16)
    d_retn = (d_mixed * swish_val).reshape(length, H, DV)
    d_ret = head_backward(d_retn, retn, hscale)
    _, pull = jax.vjp(lambda qa, ka, va: retention_full(qa, ka, va, seg), query, keys, values)
    d_query, d_keys, d_values = pull(d_ret)
    dq_half = d_query.reshape(length, QK).astype(jnp.bfloat16)
    dk_half = (d_keys * DK ** (-0.5)).reshape(length, QK).astype(jnp.bfloat16)
    dv_half = d_values.reshape(length, VW).astype(jnp.bfloat16)
    grad_query = left_contract(act_one, dq_half)
    grad_key = left_contract(act_one, dk_half)
    grad_value = left_contract(act_one, dv_half)
    grad_gate = left_contract(act_one, d_zgate)
    d_act_one = right_contract(dq_half, query_full) + right_contract(dk_half, key_full)
    d_act_one = d_act_one + right_contract(dv_half, value_full) + right_contract(d_zgate, gate_full)
    d_norm_one, grad_gain_attn = rms_backward(d_act_one, norm_one, rms_one, gain_first)
    grad_input = d_resid + d_norm_one
    grads = (grad_gain_attn, grad_query, grad_key, grad_value, grad_gate, grad_out, grad_gain_mlp, grad_up, grad_act, grad_down)
    return (block_out, grad_input, grads)

def reference(block_input, segments, cotangent, gain_attn, w_query, w_key, w_value, w_gate, w_out, gain_mlp, w_up, w_act, w_down):
    params = (gain_attn, w_query, w_key, w_value, w_gate, w_out, gain_mlp, w_up, w_act, w_down)
    inputs = block_input.reshape(NSEQ, SEQ, D)
    cots = cotangent.reshape(NSEQ, SEQ, D)
    zeros = tuple((jnp.zeros(param.shape, jnp.float32) for param in params))

    def step(carry, item):
        out_row, grad_row, grads = sequence_step(params, item[0], item[1], item[2])
        return (tuple((total + part for total, part in zip(carry, grads))), (out_row, grad_row))
    totals, (outs, grads_in) = lax.scan(step, zeros, (inputs, segments, cots))
    return (outs.reshape(TOKENS, D), grads_in.reshape(TOKENS, D), totals[0], totals[1], totals[2], totals[3], totals[4], totals[5], totals[6], totals[7], totals[8], totals[9])
```

```python
import jax
import jax.numpy as jnp
from jax import lax
from jax.sharding import PartitionSpec as P

HEADS = 4
EPS = 1e-06
HEAD_FLOOR = 1.0
HIGH = lax.Precision.HIGHEST
SQRT_HALF = 0.7071067811865476
INV_ROOT_TWO_PI = 0.3989422804014327
F32 = jnp.float32
BF16 = jnp.bfloat16


def nt(left, right):
    return lax.dot_general(left, right, (((1,), (1,)), ((), ())), preferred_element_type=F32)


def nn(left, right):
    return lax.dot_general(left, right, (((1,), (0,)), ((), ())), preferred_element_type=F32)


def tn(left, right):
    return lax.dot_general(left, right, (((0,), (0,)), ((), ())), preferred_element_type=F32)


def high_nt(left, right):
    return lax.dot_general(left, right, (((1,), (1,)), ((), ())), precision=HIGH)


def high_nn(left, right):
    return lax.dot_general(left, right, (((1,), (0,)), ((), ())), precision=HIGH)


def high_tn(left, right):
    return lax.dot_general(left, right, (((0,), (0,)), ((), ())), precision=HIGH)


def swap(value, axis, flip):
    size = lax.axis_size(axis)
    return lax.ppermute(value, axis, [(i, i ^ flip) for i in range(size)])


def xor_order(pieces, index):
    bit = 1
    while bit < len(pieces):
        hit = (index & bit) != 0
        pieces = [jnp.where(hit, pieces[k ^ bit], pieces[k]) for k in range(len(pieces))]
        bit *= 2
    return pieces


def rms(value):
    scale = lax.rsqrt(jnp.mean(value * value, axis=-1, keepdims=True) + EPS)
    return value * scale, scale


def rms_backward(d_act, normed, scale, gain):
    d_norm = d_act * gain
    return scale * (d_norm - normed * jnp.mean(d_norm * normed, axis=-1, keepdims=True))


def body(
    block_input,
    segments,
    cotangent,
    gain_attn,
    w_query,
    w_key,
    w_value,
    w_gate,
    w_out,
    gain_mlp,
    w_up,
    w_act,
    w_down,
):
    nd, ns = lax.axis_size("dp"), lax.axis_size("seq")
    d, j = lax.axis_index("dp"), lax.axis_index("seq")
    nx = 2 if nd % 2 == 0 else 1
    tokens, width = block_input.shape
    rows = w_query.shape[0]
    wide = rows * ns
    hp = HEADS // ns
    dk = w_query.shape[1] // HEADS
    dv = w_value.shape[1] // HEADS
    even = [z * nx for z in range(nd // nx)]
    odd = [z * nx + 1 for z in range(nd // nx)] if nx == 2 else []
    order = even + odd
    pair = [k for k in range(ns) if not k & 1] + [k for k in range(ns) if k & 1]

    def to_rel(value):
        parts = [value[:, a * wide : (a + 1) * wide] for a in range(nd)]
        parts = xor_order(parts, d)
        return jnp.concatenate([parts[m] for m in order], axis=1)

    def from_rel(value):
        parts = [None] * nd
        for at, m in enumerate(order):
            parts[m] = value[:, at * wide : (at + 1) * wide]
        return jnp.concatenate(xor_order(parts, d), axis=1)

    def gather_seq(own):
        got = {0: own}
        for k in range(2, ns, 2):
            got[k] = swap(own, "seq", k)
        for k in range(1, ns, 2):
            got[k] = swap(got[k - 1], "seq", 1)
        return got

    def scatter_seq(partial):
        half = partial.shape[0] // 2
        low = partial[:half] + swap(partial[half:].astype(BF16), "seq", 1).astype(F32)
        total = low[:tokens]
        for at, k in enumerate(pair[1 : ns // 2], 1):
            total = total + swap(low[at * tokens : (at + 1) * tokens].astype(BF16), "seq", k).astype(F32)
        return total

    def row(own):
        got = gather_seq(own)
        return jnp.concatenate([got[k] for k in pair], axis=0)

    tail = jnp.stack([gain_attn, gain_mlp], axis=0)
    small = jnp.concatenate([tail, segments.reshape(-1, rows).astype(BF16)], axis=0)
    small = gather_seq(small)
    seg = jnp.concatenate([small[k][2:].reshape(tokens) for k in pair], axis=0)
    gains = jnp.concatenate(xor_order([small[k][:2] for k in range(ns)], j), axis=1)
    zs = jnp.stack([gains] + [swap(gains, "dp", m) for m in even[1:]], axis=0)
    parts = [zs[i] for i in range(len(even))]
    if nx == 2:
        xs = swap(zs, "dp", 1)
        parts = parts + [xs[i] for i in range(len(even))]
    gains = jnp.concatenate(parts, axis=1).astype(F32)
    gain_first, gain_second = gains[0:1], gains[1:2]

    def own_block(mats):
        pieces = []
        for s in range(ns):
            pieces.append(jnp.concatenate([m[:, s * (m.shape[1] // ns) : (s + 1) * (m.shape[1] // ns)] for m in mats], axis=1))
        rel = xor_order(pieces, j)
        got = [rel[0]] + [swap(rel[k], "seq", k) for k in range(1, ns)]
        return jnp.concatenate(xor_order(got, j), axis=0).T

    def gather_dp(own):
        blocks = [own] + [swap(own, "dp", m) for m in even[1:]]
        if nx == 2:
            blocks = blocks + [swap(b, "dp", 1) for b in blocks]
        return jnp.concatenate(blocks, axis=1)

    def scatter_dp(left, right):
        half = len(even) * wide
        total = tn(left, right[:, :half])
        if nx == 2:
            away = tn(left, right[:, half:]).astype(BF16)
            total = total + swap(away, "dp", 1).astype(F32)
        parts = [total[:, i * wide : (i + 1) * wide] for i in range(len(even))]
        own = parts[0]
        for i in range(1, len(even)):
            own = own + swap(parts[i].astype(BF16), "dp", even[i]).astype(F32)
        return own

    def owners(block, widths):
        block = block.T.astype(BF16)
        pieces = xor_order([block[s * rows : (s + 1) * rows] for s in range(ns)], j)
        got = [pieces[0]] + [swap(pieces[k], "seq", k) for k in range(1, ns)]
        got = xor_order(got, j)
        outs, at = [], 0
        for w in widths:
            outs.append(jnp.concatenate([g[:, at : at + w] for g in got], axis=1).astype(F32))
            at += w
        return outs

    qk, vw = dk * hp, dv * hp
    fw = w_up.shape[1] // ns
    out_t, down_t = w_out.T, w_down.T
    own_a = own_block([w_query, w_key, w_value])
    own_b = own_block([w_gate, out_t])
    own_c = own_block([w_up, w_act])
    own_d = own_block([down_t])
    wa = gather_dp(own_a)
    wb = gather_dp(own_b)
    wc = gather_dp(own_c)
    wd = gather_dp(own_d)
    w_g, w_o = wb[:vw], wb[vw:]

    x = to_rel(block_input)
    cot = to_rel(cotangent)
    cot_row = row(cot.astype(BF16))

    norm_one, rms_one = rms(x)
    act_one = row((norm_one * gain_first).astype(BF16))
    qkv = nt(act_one, wa)
    zgate = nt(act_one, w_g)

    length = ns * tokens
    pos = jnp.concatenate([(j ^ k) * tokens + jnp.arange(tokens, dtype=jnp.int32) for k in pair])
    diff = pos[:, None] - pos[None, :]
    allowed = (diff >= 0) & (seg[:, None] == seg[None, :])
    span = jnp.maximum(diff, 0).astype(F32)
    heads = []
    for h in range(hp):
        head = (j * hp + h).astype(F32)
        mask = jnp.where(allowed, jnp.exp(span * jnp.log1p(-jnp.exp2(-5.0 - head))), 0.0)
        q = qkv[:, h * dk : (h + 1) * dk]
        k = qkv[:, qk + h * dk : qk + (h + 1) * dk] * dk ** (-0.5)
        v = qkv[:, 2 * qk + h * dv : 2 * qk + (h + 1) * dv]
        scores = high_nt(q, k) * mask
        ret = high_nn(scores, v)
        hscale = lax.rsqrt(jnp.mean(ret * ret, axis=-1, keepdims=True) + HEAD_FLOOR)
        heads.append((mask, q, k, v, scores, ret * hscale, hscale))
    retn = jnp.concatenate([h[5] for h in heads], axis=1)
    sig = jax.nn.sigmoid(zgate)
    swish_val, swish_slope = zgate * sig, sig * (1.0 + zgate * (1.0 - sig))
    mixed = (swish_val * retn).astype(BF16)
    resid = x + scatter_seq(nn(mixed, w_o))

    norm_two, rms_two = rms(resid)
    act_two = row((norm_two * gain_second).astype(BF16))
    both = nt(act_two, wc)
    upper, pregate = both[:, :fw], both[:, fw:]
    cdf = 0.5 * (1.0 + lax.erf(pregate * SQRT_HALF))
    dens = jnp.exp(-0.5 * pregate * pregate) * INV_ROOT_TWO_PI
    gelu_val, gelu_slope = pregate * cdf, cdf + pregate * dens
    hidden = (gelu_val * upper).astype(BF16)
    block_out = resid + scatter_seq(nn(hidden, wd))

    d_hidden = nt(cot_row, wd)
    sum_d = scatter_dp(hidden, cot_row)
    d_pre = (d_hidden * upper * gelu_slope).astype(BF16)
    d_upper = (d_hidden * gelu_val).astype(BF16)
    d_both = jnp.concatenate([d_upper, d_pre], axis=1)
    sum_c = scatter_dp(d_both, act_two)
    d_act_two = scatter_seq(nn(d_both, wc))
    d_resid = cot + rms_backward(d_act_two, norm_two, rms_two, gain_second)

    res_row = row(d_resid.astype(BF16))
    d_mixed = nt(res_row, w_o)
    d_zgate = (d_mixed * retn * swish_slope).astype(BF16)
    d_retn = d_mixed * swish_val
    sum_g = scatter_dp(d_zgate, act_one)
    sum_o = scatter_dp(mixed, res_row)
    dqs, dks, dvs = [], [], []
    for h, (mask, q, k, v, scores, rn, hscale) in enumerate(heads):
        dr = d_retn[:, h * dv : (h + 1) * dv]
        d_ret = hscale * (dr - rn * jnp.mean(dr * rn, axis=-1, keepdims=True))
        d_scores = high_nt(d_ret, v) * mask
        dqs.append(high_nn(d_scores, k).astype(BF16))
        dks.append((high_tn(d_scores, q) * dk ** (-0.5)).astype(BF16))
        dvs.append(high_tn(scores, d_ret).astype(BF16))
    d_qkv = jnp.concatenate(dqs + dks + dvs, axis=1)
    sum_a = scatter_dp(d_qkv, act_one)
    d_act_one = scatter_seq(nn(d_qkv, wa) + nn(d_zgate, w_g))
    grad_input = d_resid + rms_backward(d_act_one, norm_one, rms_one, gain_first)

    grad_query, grad_key, grad_value = owners(sum_a, [qk, qk, vw])
    (grad_gate,) = owners(sum_g, [vw])
    (grad_out,) = owners(sum_o, [vw])
    grad_up, grad_act = owners(sum_c, [fw, fw])
    (grad_down,) = owners(sum_d, [fw])

    def gain_grad(mats, grads, gain):
        total = sum(jnp.sum(m.astype(F32) * g, axis=1) for m, g in zip(mats, grads))
        return total / gain.astype(F32)

    grad_gain_attn = gain_grad(
        (w_query, w_key, w_value, w_gate), (grad_query, grad_key, grad_value, grad_gate), gain_attn
    )
    grad_gain_mlp = gain_grad((w_up, w_act), (grad_up, grad_act), gain_mlp)
    return (
        from_rel(block_out),
        from_rel(grad_input),
        grad_gain_attn,
        grad_query,
        grad_key,
        grad_value,
        grad_gate,
        grad_out.T,
        grad_gain_mlp,
        grad_up,
        grad_act,
        grad_down.T,
    )


def solution(mesh):
    both = ("dp", "seq")
    tok, vec, down, across = P(both, None), P(both), P(both, None), P(None, both)
    return jax.shard_map(
        body,
        mesh=mesh,
        in_specs=(tok, P("dp", "seq"), tok, vec, down, down, down, down, across, vec, down, down, across),
        out_specs=(tok, tok, vec, down, down, down, down, across, vec, down, down, across),
        check_vma=False,
    )
```

```python
import jax
import jax.numpy as jnp
from jax import lax
from jax.experimental import pallas as pl
from jax.experimental.pallas import tpu as pltpu
from jax.sharding import PartitionSpec as P


HEADS = 4
EPS = 1e-06
HEAD_FLOOR = 1.0
HIGH = lax.Precision.HIGHEST
SQRT_HALF = 0.7071067811865476
INV_ROOT_TWO_PI = 0.3989422804014327
F32 = jnp.float32
BF16 = jnp.bfloat16


def nt(left, right):
    return lax.dot_general(left, right, (((1,), (1,)), ((), ())), preferred_element_type=F32)


def nn(left, right):
    return lax.dot_general(left, right, (((1,), (0,)), ((), ())), preferred_element_type=F32)


def tn(left, right):
    return lax.dot_general(left, right, (((0,), (0,)), ((), ())), preferred_element_type=F32)


def high_nt(left, right):
    return lax.dot_general(left, right, (((1,), (1,)), ((), ())), precision=HIGH)


def high_nn(left, right):
    return lax.dot_general(left, right, (((1,), (0,)), ((), ())), precision=HIGH)


def high_tn(left, right):
    return lax.dot_general(left, right, (((0,), (0,)), ((), ())), precision=HIGH)


def swap(value, axis, flip, senders=None):
    size = lax.axis_size(axis)
    return lax.ppermute(value, axis, [(i, i ^ flip) for i in range(size) if senders is None or senders(i)])


def xor_order(pieces, index):
    bit = 1
    while bit < len(pieces):
        hit = (index & bit) != 0
        pieces = [jnp.where(hit, pieces[k ^ bit], pieces[k]) for k in range(len(pieces))]
        bit *= 2
    return pieces


def call(kernel, index, args, outs, scratch):
    return pl.pallas_call(
        kernel,
        out_shape=tuple(jax.ShapeDtypeStruct(*o) for o in outs),
        in_specs=[pl.BlockSpec(memory_space=pltpu.SMEM)] + [pl.BlockSpec(memory_space=pltpu.VMEM)] * len(args),
        out_specs=tuple(pl.BlockSpec(memory_space=pltpu.VMEM) for _ in outs),
        scratch_shapes=scratch,
        cost_estimate=pl.CostEstimate(flops=0, transcendentals=0, bytes_accessed=4 << 20),
    )(index.reshape(1), *args)


def cut_heads(mats, ns, j):
    rows, widths = mats[0].shape[0], [m.shape[1] // ns for m in mats]
    total = sum(widths)

    def kernel(j_ref, *refs):
        ins, outs, scr = refs[: len(mats)], refs[len(mats) : -1], refs[-1]
        for s in range(ns):
            at = 0
            for m, w in zip(ins, widths):
                scr[j_ref[0] ^ s, :, at : at + w] = m[:, s * w : (s + 1) * w]
                at += w
        for k in range(ns):
            outs[k][...] = scr[k]

    return call(kernel, j, mats, [((rows, total), BF16)] * ns, [pltpu.VMEM((ns, rows, total), BF16)])


def stack_rows(pieces, j):
    ns, (rows, total) = len(pieces), pieces[0].shape

    def kernel(j_ref, *refs):
        ins, out, scr = refs[:ns], refs[ns], refs[-1]
        for k in range(ns):
            scr[pl.ds(pl.multiple_of((j_ref[0] ^ k) * rows, rows), rows), :] = ins[k][...]
        out[...] = scr[...].T

    return call(kernel, j, pieces, [((total, rows * ns), BF16)], [pltpu.VMEM((rows * ns, total), BF16)])[0]


def cut_rows(sums, ns, j):
    wide = sums[0][0].shape[1]
    heights = [g[0].shape[0] for g in sums]
    rows, total = wide // ns, sum(heights)
    flat = [t for g in sums for t in g]

    def kernel(j_ref, *refs):
        ins, outs, scr = list(refs[: len(flat)]), refs[len(flat) : -1], refs[-1]
        at = 0
        for g, h in zip(sums, heights):
            value = ins.pop(0)[...].astype(F32)
            for _ in g[1:]:
                value = value + ins.pop(0)[...].astype(F32)
            scr[:, at : at + h] = value.T
            at += h
        for k in range(ns):
            outs[k][...] = scr[pl.ds(pl.multiple_of((j_ref[0] ^ k) * rows, rows), rows), :].astype(BF16)

    return call(kernel, j, flat, [((rows, total), BF16)] * ns, [pltpu.VMEM((wide, total), F32)])


def place_heads(pieces, widths, used, mats, extra, j):
    ns, (rows, total) = len(pieces), pieces[0].shape

    def kernel(j_ref, *refs):
        ins, w_refs = refs[:ns], refs[ns : ns + len(mats)]
        outs, scr = refs[ns + len(mats) + len(extra) : -1], refs[-1]
        for k in range(ns):
            scr[j_ref[0] ^ k] = ins[k][...].astype(F32)
        at = 0
        for out, w in zip(outs, widths):
            for s in range(ns):
                out[:, s * w : (s + 1) * w] = scr[s, :, at : at + w]
            at += w
        dots = jnp.zeros((rows, 1), F32)
        for i, m in zip(used, w_refs):
            dots = dots + jnp.sum(m[...].astype(F32) * outs[i][...], axis=1, keepdims=True)
        for e in refs[ns + len(mats) : ns + len(mats) + len(extra)]:
            dots = dots + e[...]
        outs[-1][...] = dots

    outs = [((rows, w * ns), F32) for w in widths] + [((rows, 1), F32)]
    args = list(pieces) + list(mats) + list(extra)
    return call(kernel, j, args, outs, [pltpu.VMEM((ns, rows, total), F32)])


def places(index, order, wide):
    return [
        (pl.ds(pl.multiple_of((index ^ m) * wide, wide), wide), slice(at * wide, (at + 1) * wide))
        for at, m in enumerate(order)
    ]


def to_arrival(value, index, order, wide):
    parts = [value[:, a * wide : (a + 1) * wide] for a in range(len(order))]
    parts = xor_order(parts, index)
    return jnp.concatenate([parts[m] for m in order], axis=1)


def from_arrival(value, index, order, wide):
    parts = [None] * len(order)
    for at, m in enumerate(order):
        parts[m] = value[:, at * wide : (at + 1) * wide]
    return jnp.concatenate(xor_order(parts, index), axis=1)


def enter(x, cot, d, order, wide):
    if wide % 128:
        cot = to_arrival(cot, d, order, wide)
        return to_arrival(x, d, order, wide), cot, cot.astype(BF16)

    def kernel(d_ref, x_ref, c_ref, xo, co, ch):
        for src, dst in places(d_ref[0], order, wide):
            xo[:, dst] = x_ref[:, src]
            value = c_ref[:, src]
            co[:, dst] = value
            ch[:, dst] = value.astype(BF16)

    return call(kernel, d, [x, cot], [(x.shape, F32), (x.shape, F32), (x.shape, BF16)], [])


def leave(d, order, wide, resid, low, got):
    if wide % 128:
        return from_arrival(resid + (low + got.astype(F32)), d, order, wide)

    def kernel(d_ref, r_ref, l_ref, g_ref, out):
        for dst, src in places(d_ref[0], order, wide):
            out[:, dst] = r_ref[:, src] + (l_ref[:, src] + g_ref[:, src].astype(F32))

    return call(kernel, d, [resid, low, got], [(resid.shape, F32)], [])[0]


def leave_norm(d, order, wide, d_resid, low, got, x, scale, gain):
    if wide % 128:
        back = rms_backward(low + got.astype(F32), x * scale, scale, gain)
        return from_arrival(d_resid + back, d, order, wide)

    def kernel(d_ref, r_ref, l_ref, g_ref, x_ref, s_ref, n_ref, out, scr):
        d_norm = (l_ref[...] + g_ref[...].astype(F32)) * n_ref[...]
        normed = x_ref[...] * s_ref[...]
        mean = jnp.mean(d_norm * normed, axis=-1, keepdims=True)
        scr[...] = r_ref[...] + s_ref[...] * (d_norm - normed * mean)
        for dst, src in places(d_ref[0], order, wide):
            out[:, dst] = scr[:, src]

    return call(kernel, d, [d_resid, low, got, x, scale, gain], [(x.shape, F32)], [pltpu.VMEM(x.shape, F32)])[0]


def rms(value):
    scale = lax.rsqrt(jnp.mean(value * value, axis=-1, keepdims=True) + EPS)
    return value * scale, scale


def rms_backward(d_act, normed, scale, gain):
    d_norm = d_act * gain
    return scale * (d_norm - normed * jnp.mean(d_norm * normed, axis=-1, keepdims=True))


def body(
    block_input,
    segments,
    cotangent,
    gain_attn,
    w_query,
    w_key,
    w_value,
    w_gate,
    w_out,
    gain_mlp,
    w_up,
    w_act,
    w_down,
):
    nd, ns = lax.axis_size("dp"), lax.axis_size("seq")
    d, j = lax.axis_index("dp"), lax.axis_index("seq")
    nx = 2 if nd % 2 == 0 else 1
    tokens, _ = block_input.shape
    rows = w_query.shape[0]
    wide = rows * ns
    hp = HEADS // ns
    dk = w_query.shape[1] // HEADS
    dv = w_value.shape[1] // HEADS
    even = [z * nx for z in range(nd // nx)]
    odd = [z * nx + 1 for z in range(nd // nx)] if nx == 2 else []
    order = even + odd
    pair = [k for k in range(ns) if not k & 1] + [k for k in range(ns) if k & 1]

    def gather_seq(own):
        got = {0: own}
        for k in range(2, ns, 2):
            got[k] = swap(own, "seq", k)
        for k in range(1, ns, 2):
            got[k] = swap(got[k - 1], "seq", 1)
        return got

    def scatter_seq(partial):
        half = partial.shape[0] // 2
        low = partial[:half] + swap(partial[half:].astype(BF16), "seq", 1).astype(F32)
        total = low[:tokens]
        for at, k in enumerate(pair[1 : ns // 2], 1):
            part = low[at * tokens : (at + 1) * tokens].astype(BF16)
            got = swap(part, "seq", k)
            if at < ns // 2 - 1:
                total = total + got.astype(F32)
        return total, got

    def row(own):
        got = gather_seq(own)
        return jnp.concatenate([got[k] for k in pair], axis=0)

    small = jnp.stack([gain_attn, gain_mlp], axis=0)
    small = jnp.concatenate([small, segments.reshape(-1, rows).astype(BF16)], axis=0)
    small = gather_seq(small)
    seg = jnp.concatenate([small[k][2:].reshape(tokens) for k in pair], axis=0)
    gains = jnp.concatenate(xor_order([small[k][:2] for k in range(ns)], j), axis=1)
    zs = jnp.stack([gains] + [swap(gains, "dp", m) for m in even[1:]], axis=0)
    parts = [zs[i] for i in range(len(even))]
    if nx == 2:
        xs = swap(zs, "dp", 1)
        parts = parts + [xs[i] for i in range(len(even))]
    gains = jnp.concatenate(parts, axis=1).astype(F32)
    gain_first, gain_second = gains[0:1], gains[1:2]

    def own_block(mats):
        rel = cut_heads(mats, ns, j)
        got = [rel[0]] + [swap(rel[k], "seq", k) for k in range(1, ns)]
        return stack_rows(got, j)

    def gather_dp(own):
        if len(even) == 4:
            inner = lambda i: (i // nx) in (1, 2)
            near = swap(own, "dp", nx)
            mid_a = swap(own, "dp", 3 * nx, inner)
            mid_b = swap(near, "dp", 3 * nx, inner)
            out_a = swap(mid_a, "dp", nx, inner)
            out_b = swap(mid_b, "dp", nx, inner)
            is_inner = ((d // nx) == 1) | ((d // nx) == 2)
            blocks = [own, near, jnp.where(is_inner, mid_b, out_a), jnp.where(is_inner, mid_a, out_b)]
        else:
            blocks = [own] + [swap(own, "dp", m) for m in even[1:]]
        if nx == 2:
            blocks = blocks + [swap(b, "dp", 1) for b in blocks]
        return jnp.concatenate(blocks, axis=1)

    def scatter_dp(left, right):
        terms = []
        for i, m in enumerate(even):
            got = 0.0
            if nx == 2:
                at = (len(even) + i) * wide
                away = tn(left, right[:, at : at + wide]).astype(BF16)
                got = swap(away, "dp", 1).astype(F32)
            part = tn(left, right[:, i * wide : (i + 1) * wide]) + got
            terms.append(part if i == 0 else swap(part.astype(BF16), "dp", m))
        return terms

    def to_owners(sums):
        rel = cut_rows(sums, ns, j)
        return [rel[0]] + [swap(rel[k], "seq", k) for k in range(1, ns)]

    qk, vw = dk * hp, dv * hp
    fw = w_up.shape[1] // ns
    out_t, down_t = w_out.T, w_down.T
    own_t = own_block([w_query, w_key, w_value, w_gate, out_t])
    own_m = own_block([w_up, w_act, down_t])
    wt = gather_dp(own_t)
    wm = gather_dp(own_m)
    w_in, w_o = wt[: 2 * qk + 2 * vw], wt[2 * qk + 2 * vw :]
    wc, wd = wm[: 2 * fw], wm[2 * fw :]

    x, cot, cot_half = enter(block_input, cotangent, d, order, wide)
    cot_row = row(cot_half)

    norm_one, rms_one = rms(x)
    act_one = row((norm_one * gain_first).astype(BF16))
    qkv = nt(act_one, w_in)
    zgate = qkv[:, 2 * qk + vw :]

    pos = jnp.concatenate([(j ^ k) * tokens + jnp.arange(tokens, dtype=jnp.int32) for k in pair])
    diff = pos[:, None] - pos[None, :]
    allowed = (diff >= 0) & (seg[:, None] == seg[None, :])
    span = jnp.maximum(diff, 0).astype(F32)
    heads = []
    for h in range(hp):
        head = (j * hp + h).astype(F32)
        mask = jnp.where(allowed, jnp.exp(span * jnp.log1p(-jnp.exp2(-5.0 - head))), 0.0)
        q = qkv[:, h * dk : (h + 1) * dk]
        k = qkv[:, qk + h * dk : qk + (h + 1) * dk] * dk ** (-0.5)
        v = qkv[:, 2 * qk + h * dv : 2 * qk + (h + 1) * dv]
        scores = high_nt(q, k) * mask
        ret = high_nn(scores, v)
        hscale = lax.rsqrt(jnp.mean(ret * ret, axis=-1, keepdims=True) + HEAD_FLOOR)
        heads.append((mask, q, k, v, scores, ret * hscale, hscale))
    retn = jnp.concatenate([h[5] for h in heads], axis=1)
    sig = jax.nn.sigmoid(zgate)
    swish_val, swish_slope = zgate * sig, sig * (1.0 + zgate * (1.0 - sig))
    mixed = (swish_val * retn).astype(BF16)
    low, got = scatter_seq(nn(mixed, w_o))
    resid = x + (low + got.astype(F32))

    norm_two, rms_two = rms(resid)
    act_two = row((norm_two * gain_second).astype(BF16))
    both = nt(act_two, wc)
    upper, pregate = both[:, :fw], both[:, fw:]
    cdf = 0.5 * (1.0 + lax.erf(pregate * SQRT_HALF))
    dens = jnp.exp(-0.5 * pregate * pregate) * INV_ROOT_TWO_PI
    gelu_val, gelu_slope = pregate * cdf, cdf + pregate * dens
    hidden = (gelu_val * upper).astype(BF16)
    d_hidden = nt(cot_row, wd)
    d_pre = (d_hidden * upper * gelu_slope).astype(BF16)
    d_upper = (d_hidden * gelu_val).astype(BF16)
    d_both = jnp.concatenate([d_upper, d_pre], axis=1)
    low, got = scatter_seq(nn(d_both, wc))
    sum_c = scatter_dp(d_both, act_two)
    sum_d = scatter_dp(hidden, cot_row)
    d_resid = cot + rms_backward(low + got.astype(F32), norm_two, rms_two, gain_second)

    res_half = d_resid.astype(BF16)
    res_row = row(res_half)
    late, res_row = lax.optimization_barrier((hidden, res_row))
    block_out = leave(d, order, wide, resid, *scatter_seq(nn(late, wd)))
    d_mixed = nt(res_row, w_o)
    d_zgate = (d_mixed * retn * swish_slope).astype(BF16)
    d_retn = d_mixed * swish_val
    sum_o = scatter_dp(mixed, res_row)
    dqs, dks, dvs = [], [], []
    for h, (mask, q, k, v, scores, rn, hscale) in enumerate(heads):
        dr = d_retn[:, h * dv : (h + 1) * dv]
        d_ret = hscale * (dr - rn * jnp.mean(dr * rn, axis=-1, keepdims=True))
        d_scores = high_nt(d_ret, v) * mask
        dqs.append(high_nn(d_scores, k).astype(BF16))
        dks.append((high_tn(d_scores, q) * dk ** (-0.5)).astype(BF16))
        dvs.append(high_tn(scores, d_ret).astype(BF16))
    d_in = jnp.concatenate(dqs + dks + dvs + [d_zgate], axis=1)
    sum_q = scatter_dp(d_in, act_one)
    low, got = scatter_seq(nn(d_in, w_in))
    grad_input = leave_norm(d, order, wide, d_resid, low, got, x, rms_one, gain_first)

    got = to_owners([sum_c, sum_d])
    grad_up, grad_act, grad_down, dots_mlp = place_heads(got, [fw] * 3, [0, 1], [w_up, w_act], [], j)
    got = to_owners([sum_o])
    grad_out, _ = place_heads(got, [vw], [], [], [], j)
    got = to_owners([sum_q])
    grad_query, grad_key, grad_value, grad_gate, dots_attn = place_heads(
        got, [qk, qk, vw, vw], [0, 1, 2, 3], [w_query, w_key, w_value, w_gate], [], j
    )
    grad_gain_attn = dots_attn.reshape(rows) / gain_attn.astype(F32)
    grad_gain_mlp = dots_mlp.reshape(rows) / gain_mlp.astype(F32)
    return (
        block_out,
        grad_input,
        grad_gain_attn,
        grad_query,
        grad_key,
        grad_value,
        grad_gate,
        grad_out.T,
        grad_gain_mlp,
        grad_up,
        grad_act,
        grad_down.T,
    )


def solution(mesh):
    both = ("dp", "seq")
    tok, vec, down, across = P(both, None), P(both), P(both, None), P(None, both)

    return jax.shard_map(
        body,
        mesh=mesh,
        in_specs=(tok, P("dp", "seq"), tok, vec, down, down, down, down, across, vec, down, down, across),
        out_specs=(tok, tok, vec, down, down, down, down, across, vec, down, down, across),
        check_vma=False,
    )
```

```python
import jax
import jax.numpy as jnp
from jax import lax
from jax.experimental import pallas as pl
from jax.experimental.pallas import tpu as pltpu
from jax.sharding import PartitionSpec as P


HEADS = 4
EPS = 1e-06
HEAD_FLOOR = 1.0
HIGH = lax.Precision.HIGH
SQRT_HALF = 0.7071067811865476
INV_ROOT_TWO_PI = 0.3989422804014327
F32 = jnp.float32
BF16 = jnp.bfloat16
DP, SEQ = "dp", "seq"


def nt(left, right):
    return lax.dot_general(left, right, (((1,), (1,)), ((), ())), preferred_element_type=F32)


def nn(left, right):
    return lax.dot_general(left, right, (((1,), (0,)), ((), ())), preferred_element_type=F32)


def tn(left, right):
    return lax.dot_general(left, right, (((0,), (0,)), ((), ())), preferred_element_type=F32)


def high_nt(left, right):
    return lax.dot_general(left, right, (((1,), (1,)), ((), ())), precision=HIGH)


def high_nn(left, right):
    return lax.dot_general(left, right, (((1,), (0,)), ((), ())), precision=HIGH)


def high_tn(left, right):
    return lax.dot_general(left, right, (((0,), (0,)), ((), ())), precision=HIGH)


def swap(value, axis, flip):
    size = lax.axis_size(axis)
    return lax.ppermute(value, axis, [(i, i ^ flip) for i in range(size)])


def swap_inner(value, flip, inner):
    nd, ns = lax.axis_size(DP), lax.axis_size(SEQ)
    pairs = [(i * ns + k, (i ^ flip) * ns + k if inner(i) else i * ns + (k ^ 1)) for i in range(nd) for k in range(ns)]
    return lax.ppermute(value, (DP, SEQ), pairs)


def xor_order(pieces, index):
    bit = 1
    while bit < len(pieces):
        hit = (index & bit) != 0
        pieces = [jnp.where(hit, pieces[k ^ bit], pieces[k]) for k in range(len(pieces))]
        bit *= 2
    return pieces


def call(kernel, index, args, outs, scratch):
    def size(shape, dtype):
        full = -(-shape[-1] // 128) * 128 * -(-shape[-2] // 16) * 16
        for n in shape[:-2]:
            full *= n
        return full * jnp.dtype(dtype).itemsize

    total = sum(size(a.shape, a.dtype) for a in args) + sum(size(*o) for o in outs)
    total += sum(size(m.shape, m.dtype) for m in scratch)
    return pl.pallas_call(
        kernel,
        out_shape=tuple(jax.ShapeDtypeStruct(*o) for o in outs),
        in_specs=[pl.BlockSpec(memory_space=pltpu.SMEM)] + [pl.BlockSpec(memory_space=pltpu.VMEM)] * len(args),
        out_specs=tuple(pl.BlockSpec(memory_space=pltpu.VMEM) for _ in outs),
        scratch_shapes=scratch,
        cost_estimate=pl.CostEstimate(flops=0, transcendentals=0, bytes_accessed=4 << 20),
        compiler_params=pltpu.CompilerParams(vmem_limit_bytes=total + total // 2 + (3 << 20)),
    )(index.reshape(1), *args)


def cut_heads(mats, ns, j):
    rows, widths = mats[0].shape[0], [m.shape[1] // ns for m in mats]
    total = sum(widths)

    def kernel(j_ref, *refs):
        ins, outs, scr = refs[: len(mats)], refs[len(mats) : -1], refs[-1]
        for s in range(ns):
            at = 0
            for m, w in zip(ins, widths):
                scr[j_ref[0] ^ s, :, at : at + w] = m[:, s * w : (s + 1) * w]
                at += w
        for k in range(ns):
            outs[k][...] = scr[k]

    return call(kernel, j, mats, [((rows, total), BF16)] * ns, [pltpu.VMEM((ns, rows, total), BF16)])


def cut_heads_whole(mats, ns, j):
    rows, widths = mats[0].shape[0], [m.shape[1] // ns for m in mats]

    def kernel(j_ref, *refs):
        ins, out = refs[:-1], refs[-1]
        for s in range(ns):
            at = 0
            for m, w in zip(ins, widths):
                out[j_ref[0] ^ s, :, at : at + w] = m[:, s * w : (s + 1) * w]
                at += w

    return call(kernel, j, mats, [((ns, rows, sum(widths)), BF16)], [])[0]


def pair_up(first, second, j):
    ns, rows, total = first.shape

    def kernel(j_ref, a_ref, b_ref, *outs):
        for k in range(ns):
            outs[k][:rows] = a_ref[k]
            outs[k][rows:] = b_ref[k]

    return call(kernel, j, [first, second], [((2 * rows, total), BF16)] * ns, [])


def stack_rows(pieces, rows, heights, j, joint=0):
    ns, (tall, total) = len(pieces), pieces[0].shape
    groups = tall // rows

    def kernel(j_ref, *refs):
        ins, outs, scr = refs[:ns], list(refs[ns:-1]), refs[-1]
        for g in range(groups):
            for k in range(ns):
                at = pl.ds(pl.multiple_of((j_ref[0] ^ k) * rows, rows), rows)
                scr[at, :] = ins[k][g * rows : (g + 1) * rows]
            value, at = scr[...].T, 0
            for h in heights:
                outs.pop(0)[...] = value[at : at + h]
                at += h
            if joint:
                outs[-1][g] = value[at : at + joint]

    outs = [((h, rows * ns), BF16) for _ in range(groups) for h in heights]
    if joint:
        outs.append(((groups, joint, rows * ns), BF16))
    return call(kernel, j, pieces, outs, [pltpu.VMEM((rows * ns, total), BF16)])


def cut_rows(sums, ns, j):
    wide = sums[0][0].shape[1]
    heights = [g[0].shape[0] for g in sums]
    rows, total = wide // ns, sum(heights)
    flat = [t for g in sums for t in g]

    def kernel(j_ref, *refs):
        ins, outs, scr = list(refs[: len(flat)]), refs[len(flat) : -1], refs[-1]
        at = 0
        for g, h in zip(sums, heights):
            value = ins.pop(0)[...].astype(F32)
            for _ in g[1:]:
                value = value + ins.pop(0)[...].astype(F32)
            scr[:, at : at + h] = value.T
            at += h
        for k in range(ns):
            outs[k][...] = scr[pl.ds(pl.multiple_of((j_ref[0] ^ k) * rows, rows), rows), :].astype(BF16)

    return call(kernel, j, flat, [((rows, total), BF16)] * ns, [pltpu.VMEM((wide, total), F32)])


def place_heads(pieces, widths, used, mats, extra, j):
    ns, (rows, total) = len(pieces), pieces[0].shape

    def kernel(j_ref, *refs):
        ins, w_refs = refs[:ns], refs[ns : ns + len(mats)]
        outs, scr = refs[ns + len(mats) + len(extra) : -1], refs[-1]
        for k in range(ns):
            scr[j_ref[0] ^ k] = ins[k][...].astype(F32)
        at = 0
        for out, w in zip(outs, widths):
            for s in range(ns):
                out[:, s * w : (s + 1) * w] = scr[s, :, at : at + w]
            at += w
        dots = jnp.zeros((rows, 1), F32)
        for i, m in zip(used, w_refs):
            dots = dots + jnp.sum(m[...].astype(F32) * outs[i][...], axis=1, keepdims=True)
        for e in refs[ns + len(mats) : ns + len(mats) + len(extra)]:
            dots = dots + e[...]
        outs[-1][...] = dots

    outs = [((rows, w * ns), F32) for w in widths] + [((rows, 1), F32)]
    args = list(pieces) + list(mats) + list(extra)
    return call(kernel, j, args, outs, [pltpu.VMEM((ns, rows, total), F32)])


def places(index, order, wide):
    return [
        (pl.ds(pl.multiple_of((index ^ m) * wide, wide), wide), slice(at * wide, (at + 1) * wide))
        for at, m in enumerate(order)
    ]


def to_arrival(value, index, order, wide):
    parts = [value[:, a * wide : (a + 1) * wide] for a in range(len(order))]
    parts = xor_order(parts, index)
    return jnp.concatenate([parts[m] for m in order], axis=1)


def from_arrival(value, index, order, wide):
    parts = [None] * len(order)
    for at, m in enumerate(order):
        parts[m] = value[:, at * wide : (at + 1) * wide]
    return jnp.concatenate(xor_order(parts, index), axis=1)


def enter(x, cot, d, order, wide):
    if wide % 128:
        cot = to_arrival(cot, d, order, wide)
        return to_arrival(x, d, order, wide), cot, cot.astype(BF16)

    def kernel(d_ref, x_ref, c_ref, xo, co, ch):
        for src, dst in places(d_ref[0], order, wide):
            xo[:, dst] = x_ref[:, src]
            value = c_ref[:, src]
            co[:, dst] = value
            ch[:, dst] = value.astype(BF16)

    return call(kernel, d, [x, cot], [(x.shape, F32), (x.shape, F32), (x.shape, BF16)], [])


def leave(d, order, wide, resid, low, got):
    if wide % 128:
        return from_arrival(resid + (low + got.astype(F32)), d, order, wide)

    def kernel(d_ref, r_ref, l_ref, g_ref, out):
        for dst, src in places(d_ref[0], order, wide):
            out[:, dst] = r_ref[:, src] + (l_ref[:, src] + g_ref[:, src].astype(F32))

    return call(kernel, d, [resid, low, got], [(resid.shape, F32)], [])[0]


def leave_norm(d, order, wide, d_resid, low, got, x, scale, gain):
    if wide % 128:
        back = rms_backward(low + got.astype(F32), x * scale, scale, gain)
        return from_arrival(d_resid + back, d, order, wide)

    def kernel(d_ref, r_ref, l_ref, g_ref, x_ref, s_ref, n_ref, out, scr):
        d_norm = (l_ref[...] + g_ref[...].astype(F32)) * n_ref[...]
        normed = x_ref[...] * s_ref[...]
        mean = jnp.mean(d_norm * normed, axis=-1, keepdims=True)
        scr[...] = r_ref[...] + s_ref[...] * (d_norm - normed * mean)
        for dst, src in places(d_ref[0], order, wide):
            out[:, dst] = scr[:, src]

    return call(kernel, d, [d_resid, low, got, x, scale, gain], [(x.shape, F32)], [pltpu.VMEM(x.shape, F32)])[0]


def rms(value):
    scale = lax.rsqrt(jnp.mean(value * value, axis=-1, keepdims=True) + EPS)
    return value * scale, scale


def rms_backward(d_act, normed, scale, gain):
    d_norm = d_act * gain
    return scale * (d_norm - normed * jnp.mean(d_norm * normed, axis=-1, keepdims=True))


def body(
    block_input,
    segments,
    cotangent,
    gain_attn,
    w_query,
    w_key,
    w_value,
    w_gate,
    w_out,
    gain_mlp,
    w_up,
    w_act,
    w_down,
):
    nd, ns = lax.axis_size(DP), lax.axis_size(SEQ)
    d, j = lax.axis_index(DP), lax.axis_index(SEQ)
    nx = 2 if nd % 2 == 0 else 1
    tokens, _ = block_input.shape
    rows = w_query.shape[0]
    wide = rows * ns
    hp = HEADS // ns
    dk = w_query.shape[1] // HEADS
    dv = w_value.shape[1] // HEADS
    even = [z * nx for z in range(nd // nx)]
    odd = [z * nx + 1 for z in range(nd // nx)] if nx == 2 else []
    order = even + odd
    pair = [k for k in range(ns) if not k & 1] + [k for k in range(ns) if k & 1]

    def gather_seq(own):
        got = {0: own}
        for k in range(2, ns, 2):
            got[k] = swap(own, SEQ, k)
        for k in range(1, ns, 2):
            got[k] = swap(got[k - 1], SEQ, 1)
        return got

    def scatter_seq(partial):
        half = partial.shape[0] // 2
        low = partial[:half] + swap(partial[half:].astype(BF16), SEQ, 1).astype(F32)
        total = low[:tokens]
        for at, k in enumerate(pair[1 : ns // 2], 1):
            part = low[at * tokens : (at + 1) * tokens].astype(BF16)
            got = swap(part, SEQ, k)
            if at < ns // 2 - 1:
                total = total + got.astype(F32)
        return total, got

    def row(own):
        got = gather_seq(own)
        return jnp.concatenate([got[k] for k in pair], axis=0)

    small = jnp.stack([gain_attn, gain_mlp], axis=0)
    small = jnp.concatenate([small, segments.reshape(-1, rows).astype(BF16)], axis=0)
    small = gather_seq(small)
    seg = jnp.concatenate([small[k][2:].reshape(tokens) for k in pair], axis=0)
    gains = jnp.concatenate(xor_order([small[k][:2] for k in range(ns)], j), axis=1)
    zs = [gains] + [swap(gains, DP, m) for m in even[1:]]
    zs = jnp.stack(zs, axis=0)
    parts = [zs[i] for i in range(len(even))]
    if nx == 2:
        xs = swap(zs, DP, 1)
        parts = parts + [xs[i] for i in range(len(even))]
    gains = jnp.concatenate(parts, axis=1).astype(F32)
    gain_first, gain_second = gains[0:1], gains[1:2]

    def own_block(mats):
        rel = cut_heads(mats, ns, j)
        got = [rel[0]] + [swap(rel[k], SEQ, k) for k in range(1, ns)]
        height = sum(m.shape[1] // ns for m in mats)
        return stack_rows(got, rows, [height], j)

    def own_blocks(groups, late):
        mats = [m for g in groups for m in g] + late
        heights = [sum(m.shape[1] // ns for m in g) for g in groups]
        whole = cut_heads_whole(mats, ns, j)
        if nx == 2:
            rel = pair_up(whole, swap(whole, DP, 1), j)
        else:
            rel = [whole[k] for k in range(ns)]
        got = [rel[0]] + [swap(rel[k], SEQ, k) for k in range(1, ns)]
        got = stack_rows(got, rows, heights, j, sum(m.shape[1] // ns for m in late))
        return [got[i : -1 : len(groups)] for i in range(len(groups))] + [got[-1]]

    def along(own):
        if len(even) != 4:
            return [own] + [swap(own, DP, m) for m in even[1:]]
        inner = lambda i: (i // nx) in (1, 2)
        near = swap(own, DP, nx)
        mid_a = swap_inner(own, 3 * nx, inner)
        mid_b = swap_inner(near, 3 * nx, inner)
        out_a = swap(mid_a, DP, nx)
        out_b = swap(mid_b, DP, nx)
        is_inner = ((d // nx) == 1) | ((d // nx) == 2)
        return [own, near, jnp.where(is_inner, mid_b, out_a), jnp.where(is_inner, mid_a, out_b)]

    def gather_dp(own):
        own, across = own[0], own[1:]
        blocks = along(own)
        if nx == 2:
            more = [swap(b, DP, 1) for i, b in enumerate(blocks) if i or not across]
            blocks = blocks + list(across) + more
        return jnp.concatenate(blocks, axis=1)

    def gather_dp_late(own):
        blocks = along(own)
        return jnp.concatenate([b[i] for i in range(nx) for b in blocks], axis=1)

    def reduce_line(part, stepwise):
        if stepwise and len(even) == 4:
            inner = lambda i: (i // nx) in (1, 2)

            def add(value, got):
                return (value.astype(F32) + got.astype(F32)).astype(BF16)

            third, second = part(3).astype(BF16), part(2).astype(BF16)
            in_b = swap(third, DP, nx)
            in_a = swap(second, DP, nx)
            second = add(second, in_b)
            mid_d = swap_inner(second, 3 * nx, inner)
            third = add(third, in_a)
            mid_c = swap_inner(third, 3 * nx, inner)
            is_inner = ((d // nx) == 1) | ((d // nx) == 2)
            first = add(part(1), jnp.where(is_inner, mid_d, 0))
            return [part(0), jnp.where(is_inner, mid_c, 0), swap(first, DP, nx)]
        far = range(1, len(even))
        return [part(0)] + [swap(part(i).astype(BF16), DP, even[i]) for i in far]

    def block_of(value, m):
        at = order.index(m)
        return value[:, at * wide : (at + 1) * wide]

    def scatter_dp(left, right, name):
        def part(i):
            got = 0.0
            if nx == 2:
                away = tn(left, block_of(right, even[i] + 1)).astype(BF16)
                got = swap(away, DP, 1).astype(F32)
            return tn(left, block_of(right, even[i])) + got

        return reduce_line(part, name in STEPWISE)

    def scatter_dp_late(left, right, name):
        def part(i):
            near = tn(left, block_of(right, even[i]))
            if nx == 1:
                return near[None]
            far = tn(left, block_of(right, even[i] + 1))
            return jnp.stack([near, far], axis=0)

        terms = reduce_line(part, name in STEPWISE)
        total = sum(t.astype(F32) for t in terms)
        own, away = total[0], total[nx - 1].astype(BF16)
        return [own, swap(away, DP, 1)] if nx == 2 else [own]

    def to_owners(sums):
        rel = cut_rows(sums, ns, j)
        return [rel[0]] + [swap(rel[k], SEQ, k) for k in range(1, ns)]

    qk, vw = dk * hp, dv * hp
    fw = w_up.shape[1] // ns
    out_t, down_t = w_out.T, w_down.T
    own_t = own_block([w_query, w_key, w_value, w_gate])
    own_o, own_m, own_d = own_blocks([[out_t], [w_up, w_act]], [down_t])
    w_in = gather_dp(own_t)
    w_o = gather_dp(own_o)
    wc = gather_dp(own_m)
    wd = gather_dp_late(own_d)

    x, cot, cot_half = enter(block_input, cotangent, d, order, wide)
    cot_row = row(cot_half)

    norm_one, rms_one = rms(x)
    act_one = row((norm_one * gain_first).astype(BF16))
    qkv = nt(act_one, w_in)
    zgate = qkv[:, 2 * qk + vw :]

    pos = jnp.concatenate([(j ^ k) * tokens + jnp.arange(tokens, dtype=jnp.int32) for k in pair])
    diff = pos[:, None] - pos[None, :]
    allowed = (diff >= 0) & (seg[:, None] == seg[None, :])
    span = jnp.maximum(diff, 0).astype(F32)
    heads = []
    for h in range(hp):
        head = (j * hp + h).astype(F32)
        mask = jnp.where(allowed, jnp.exp(span * jnp.log1p(-jnp.exp2(-5.0 - head))), 0.0)
        q = qkv[:, h * dk : (h + 1) * dk]
        k = qkv[:, qk + h * dk : qk + (h + 1) * dk] * dk ** (-0.5)
        v = qkv[:, 2 * qk + h * dv : 2 * qk + (h + 1) * dv]
        scores = high_nt(q, k) * mask
        ret = high_nn(scores, v)
        hscale = lax.rsqrt(jnp.mean(ret * ret, axis=-1, keepdims=True) + HEAD_FLOOR)
        heads.append((mask, q, k, v, scores, ret * hscale, hscale))
    retn = jnp.concatenate([h[5] for h in heads], axis=1)
    sig = jax.nn.sigmoid(zgate)
    swish_val, swish_slope = zgate * sig, sig * (1.0 + zgate * (1.0 - sig))
    mixed = (swish_val * retn).astype(BF16)
    low, got = scatter_seq(nn(mixed, w_o))
    resid = x + (low + got.astype(F32))

    norm_two, rms_two = rms(resid)
    act_two = (norm_two * gain_second).astype(BF16)
    act_two = row(act_two)
    both = nt(act_two, wc)
    upper, pregate = both[:, :fw], both[:, fw:]
    cdf = 0.5 * (1.0 + lax.erf(pregate * SQRT_HALF))
    dens = jnp.exp(-0.5 * pregate * pregate) * INV_ROOT_TWO_PI
    gelu_val, gelu_slope = pregate * cdf, cdf + pregate * dens
    hidden = (gelu_val * upper).astype(BF16)
    d_hidden = nt(cot_row, wd)
    d_pre = (d_hidden * upper * gelu_slope).astype(BF16)
    d_upper = (d_hidden * gelu_val).astype(BF16)
    d_both = jnp.concatenate([d_upper, d_pre], axis=1)
    low, got = scatter_seq(nn(d_both, wc))
    sum_c = scatter_dp(d_both, act_two, "C")
    sum_d = scatter_dp_late(hidden, cot_row, "D")
    d_resid = cot + rms_backward(low + got.astype(F32), norm_two, rms_two, gain_second)

    res_half = d_resid.astype(BF16)
    res_row = row(res_half)
    late, res_row = lax.optimization_barrier((hidden, res_row))
    block_out = leave(d, order, wide, resid, *scatter_seq(nn(late, wd)))
    sum_o = scatter_dp(mixed, res_row, "O")
    d_mixed = nt(res_row, w_o)
    d_zgate = (d_mixed * retn * swish_slope).astype(BF16)
    d_retn = d_mixed * swish_val
    dqs, dks, dvs = [], [], []
    for h, (mask, q, k, v, scores, rn, hscale) in enumerate(heads):
        dr = d_retn[:, h * dv : (h + 1) * dv]
        d_ret = hscale * (dr - rn * jnp.mean(dr * rn, axis=-1, keepdims=True))
        d_scores = high_nt(d_ret, v) * mask
        dqs.append(high_nn(d_scores, k).astype(BF16))
        dks.append((high_tn(d_scores, q) * dk ** (-0.5)).astype(BF16))
        dvs.append(high_tn(scores, d_ret).astype(BF16))
    d_in = jnp.concatenate(dqs + dks + dvs + [d_zgate], axis=1)
    sum_q = scatter_dp(d_in, act_one, "Q")
    d_act_one = nn(d_in, w_in)
    low, got = scatter_seq(d_act_one)
    grad_input = leave_norm(d, order, wide, d_resid, low, got, x, rms_one, gain_first)

    got = to_owners([sum_c, sum_d, sum_o])
    grad_up, grad_act, grad_down, grad_out, dots_mlp = place_heads(got, [fw, fw, fw, vw], [0, 1], [w_up, w_act], [], j)
    got = to_owners([sum_q])
    grad_query, grad_key, grad_value, grad_gate, dots_attn = place_heads(
        got, [qk, qk, vw, vw], [0, 1, 2, 3], [w_query, w_key, w_value, w_gate], [], j
    )
    grad_gain_attn = dots_attn.reshape(rows) / gain_attn.astype(F32)
    grad_gain_mlp = dots_mlp.reshape(rows) / gain_mlp.astype(F32)
    return (
        block_out,
        grad_input,
        grad_gain_attn,
        grad_query,
        grad_key,
        grad_value,
        grad_gate,
        grad_out.T,
        grad_gain_mlp,
        grad_up,
        grad_act,
        grad_down.T,
    )


STEPWISE = "CDOQ"


def solution(mesh):
    both = (DP, SEQ)
    tok, vec, down, across = P(both, None), P(both), P(both, None), P(None, both)

    return jax.shard_map(
        body,
        mesh=mesh,
        in_specs=(tok, P(DP, SEQ), tok, vec, down, down, down, down, across, vec, down, down, across),
        out_specs=(tok, tok, vec, down, down, down, down, across, vec, down, down, across),
        check_vma=False,
    )
```

```python
import jax
import jax.numpy as jnp
from jax import lax
from jax.experimental import pallas as pl
from jax.experimental.pallas import tpu as pltpu
from jax.sharding import PartitionSpec as P


HEADS = 4
EPS = 1e-06
HEAD_FLOOR = 1.0
HIGH = lax.Precision.HIGH
SQRT_HALF = 0.7071067811865476
INV_ROOT_TWO_PI = 0.3989422804014327
F32 = jnp.float32
BF16 = jnp.bfloat16
DP, SEQ = "dp", "seq"


def nt(left, right):
    return lax.dot_general(left, right, (((1,), (1,)), ((), ())), preferred_element_type=F32)


def nn(left, right):
    return lax.dot_general(left, right, (((1,), (0,)), ((), ())), preferred_element_type=F32)


def tn(left, right):
    return lax.dot_general(left, right, (((0,), (0,)), ((), ())), preferred_element_type=F32)


def high_nt(left, right):
    return lax.dot_general(left, right, (((1,), (1,)), ((), ())), precision=HIGH)


def high_nn(left, right):
    return lax.dot_general(left, right, (((1,), (0,)), ((), ())), precision=HIGH)


def high_tn(left, right):
    return lax.dot_general(left, right, (((0,), (0,)), ((), ())), precision=HIGH)


def swap(value, axis, flip):
    size = lax.axis_size(axis)
    return lax.ppermute(value, axis, [(i, i ^ flip) for i in range(size)])


def swap_inner(value, flip, inner):
    nd, ns = lax.axis_size(DP), lax.axis_size(SEQ)
    pairs = [(i * ns + k, (i ^ flip) * ns + k if inner(i) else i * ns + (k ^ 1)) for i in range(nd) for k in range(ns)]
    return lax.ppermute(value, (DP, SEQ), pairs)


def xor_order(pieces, index):
    bit = 1
    while bit < len(pieces):
        hit = (index & bit) != 0
        pieces = [jnp.where(hit, pieces[k ^ bit], pieces[k]) for k in range(len(pieces))]
        bit *= 2
    return pieces


def call(kernel, index, args, outs, scratch):
    def size(shape, dtype):
        full = -(-shape[-1] // 128) * 128 * -(-shape[-2] // 16) * 16
        for n in shape[:-2]:
            full *= n
        return full * jnp.dtype(dtype).itemsize

    total = sum(size(a.shape, a.dtype) for a in args) + sum(size(*o) for o in outs)
    total += sum(size(m.shape, m.dtype) for m in scratch)
    return pl.pallas_call(
        kernel,
        out_shape=tuple(jax.ShapeDtypeStruct(*o) for o in outs),
        in_specs=[pl.BlockSpec(memory_space=pltpu.SMEM)] + [pl.BlockSpec(memory_space=pltpu.VMEM)] * len(args),
        out_specs=tuple(pl.BlockSpec(memory_space=pltpu.VMEM) for _ in outs),
        scratch_shapes=scratch,
        cost_estimate=pl.CostEstimate(flops=0, transcendentals=0, bytes_accessed=4 << 20),
        compiler_params=pltpu.CompilerParams(vmem_limit_bytes=total + total // 2 + (3 << 20)),
    )(index.reshape(1), *args)


def cut_heads(mats, ns, j):
    rows, widths = mats[0].shape[0], [m.shape[1] // ns for m in mats]
    total = sum(widths)

    def kernel(j_ref, *refs):
        ins, outs, scr = refs[: len(mats)], refs[len(mats) : -1], refs[-1]
        for s in range(ns):
            at = 0
            for m, w in zip(ins, widths):
                scr[j_ref[0] ^ s, :, at : at + w] = m[:, s * w : (s + 1) * w]
                at += w
        for k in range(ns):
            outs[k][...] = scr[k]

    return call(kernel, j, mats, [((rows, total), BF16)] * ns, [pltpu.VMEM((ns, rows, total), BF16)])


def cut_heads_whole(mats, ns, j):
    rows, widths = mats[0].shape[0], [m.shape[1] // ns for m in mats]

    def kernel(j_ref, *refs):
        ins, out = refs[:-1], refs[-1]
        for s in range(ns):
            at = 0
            for m, w in zip(ins, widths):
                out[j_ref[0] ^ s, :, at : at + w] = m[:, s * w : (s + 1) * w]
                at += w

    return call(kernel, j, mats, [((ns, rows, sum(widths)), BF16)], [])[0]


def pair_up(first, second, j):
    ns, rows, total = first.shape

    def kernel(j_ref, a_ref, b_ref, *outs):
        for k in range(ns):
            outs[k][:rows] = a_ref[k]
            outs[k][rows:] = b_ref[k]

    return call(kernel, j, [first, second], [((2 * rows, total), BF16)] * ns, [])


def stack_rows(pieces, rows, heights, j, joint=0):
    ns, (tall, total) = len(pieces), pieces[0].shape
    groups = tall // rows

    def kernel(j_ref, *refs):
        ins, outs, scr = refs[:ns], list(refs[ns:-1]), refs[-1]
        for g in range(groups):
            for k in range(ns):
                at = pl.ds(pl.multiple_of((j_ref[0] ^ k) * rows, rows), rows)
                scr[at, :] = ins[k][g * rows : (g + 1) * rows]
            value, at = scr[...].T, 0
            for h in heights:
                outs.pop(0)[...] = value[at : at + h]
                at += h
            if joint:
                outs[-1][g] = value[at : at + joint]

    outs = [((h, rows * ns), BF16) for _ in range(groups) for h in heights]
    if joint:
        outs.append(((groups, joint, rows * ns), BF16))
    return call(kernel, j, pieces, outs, [pltpu.VMEM((rows * ns, total), BF16)])


def cut_rows(sums, ns, j):
    wide = sums[0][0].shape[1]
    heights = [g[0].shape[0] for g in sums]
    rows, total = wide // ns, sum(heights)
    flat = [t for g in sums for t in g]

    def kernel(j_ref, *refs):
        ins, outs, scr = list(refs[: len(flat)]), refs[len(flat) : -1], refs[-1]
        at = 0
        for g, h in zip(sums, heights):
            value = ins.pop(0)[...].astype(F32)
            for _ in g[1:]:
                value = value + ins.pop(0)[...].astype(F32)
            scr[:, at : at + h] = value.T
            at += h
        for k in range(ns):
            outs[k][...] = scr[pl.ds(pl.multiple_of((j_ref[0] ^ k) * rows, rows), rows), :].astype(BF16)

    return call(kernel, j, flat, [((rows, total), BF16)] * ns, [pltpu.VMEM((wide, total), F32)])


def place_heads(pieces, widths, used, mats, extra, j):
    ns, (rows, total) = len(pieces), pieces[0].shape

    def kernel(j_ref, *refs):
        ins, w_refs = refs[:ns], refs[ns : ns + len(mats)]
        outs, scr = refs[ns + len(mats) + len(extra) : -1], refs[-1]
        for k in range(ns):
            scr[j_ref[0] ^ k] = ins[k][...].astype(F32)
        at = 0
        for out, w in zip(outs, widths):
            for s in range(ns):
                out[:, s * w : (s + 1) * w] = scr[s, :, at : at + w]
            at += w
        dots = jnp.zeros((rows, 1), F32)
        for i, m in zip(used, w_refs):
            dots = dots + jnp.sum(m[...].astype(F32) * outs[i][...], axis=1, keepdims=True)
        for e in refs[ns + len(mats) : ns + len(mats) + len(extra)]:
            dots = dots + e[...]
        outs[-1][...] = dots

    outs = [((rows, w * ns), F32) for w in widths] + [((rows, 1), F32)]
    args = list(pieces) + list(mats) + list(extra)
    return call(kernel, j, args, outs, [pltpu.VMEM((ns, rows, total), F32)])


def places(index, order, wide):
    return [
        (pl.ds(pl.multiple_of((index ^ m) * wide, wide), wide), slice(at * wide, (at + 1) * wide))
        for at, m in enumerate(order)
    ]


def to_arrival(value, index, order, wide):
    parts = [value[:, a * wide : (a + 1) * wide] for a in range(len(order))]
    parts = xor_order(parts, index)
    return jnp.concatenate([parts[m] for m in order], axis=1)


def from_arrival(value, index, order, wide):
    parts = [None] * len(order)
    for at, m in enumerate(order):
        parts[m] = value[:, at * wide : (at + 1) * wide]
    return jnp.concatenate(xor_order(parts, index), axis=1)


def enter(x, cot, d, order, wide):
    if wide % 128:
        cot = to_arrival(cot, d, order, wide)
        return to_arrival(x, d, order, wide), cot, cot.astype(BF16)

    def kernel(d_ref, x_ref, c_ref, xo, co, ch):
        for src, dst in places(d_ref[0], order, wide):
            xo[:, dst] = x_ref[:, src]
            value = c_ref[:, src]
            co[:, dst] = value
            ch[:, dst] = value.astype(BF16)

    return call(kernel, d, [x, cot], [(x.shape, F32), (x.shape, F32), (x.shape, BF16)], [])


def leave(d, order, wide, resid, low, got):
    if wide % 128:
        return from_arrival(resid + (low + got.astype(F32)), d, order, wide)

    def kernel(d_ref, r_ref, l_ref, g_ref, out):
        for dst, src in places(d_ref[0], order, wide):
            out[:, dst] = r_ref[:, src] + (l_ref[:, src] + g_ref[:, src].astype(F32))

    return call(kernel, d, [resid, low, got], [(resid.shape, F32)], [])[0]


def leave_norm(d, order, wide, d_resid, low, got, x, scale, gain):
    if wide % 128:
        back = rms_backward(low + got.astype(F32), x * scale, scale, gain)
        return from_arrival(d_resid + back, d, order, wide)

    def kernel(d_ref, r_ref, l_ref, g_ref, x_ref, s_ref, n_ref, out, scr):
        d_norm = (l_ref[...] + g_ref[...].astype(F32)) * n_ref[...]
        normed = x_ref[...] * s_ref[...]
        mean = jnp.mean(d_norm * normed, axis=-1, keepdims=True)
        scr[...] = r_ref[...] + s_ref[...] * (d_norm - normed * mean)
        for dst, src in places(d_ref[0], order, wide):
            out[:, dst] = scr[:, src]

    return call(kernel, d, [d_resid, low, got, x, scale, gain], [(x.shape, F32)], [pltpu.VMEM(x.shape, F32)])[0]


def rms(value):
    scale = lax.rsqrt(jnp.mean(value * value, axis=-1, keepdims=True) + EPS)
    return value * scale, scale


def rms_backward(d_act, normed, scale, gain):
    d_norm = d_act * gain
    return scale * (d_norm - normed * jnp.mean(d_norm * normed, axis=-1, keepdims=True))


def body(
    block_input,
    segments,
    cotangent,
    gain_attn,
    w_query,
    w_key,
    w_value,
    w_gate,
    w_out,
    gain_mlp,
    w_up,
    w_act,
    w_down,
):
    nd, ns = lax.axis_size(DP), lax.axis_size(SEQ)
    d, j = lax.axis_index(DP), lax.axis_index(SEQ)
    nx = 2 if nd % 2 == 0 else 1
    tokens, _ = block_input.shape
    rows = w_query.shape[0]
    wide = rows * ns
    hp = HEADS // ns
    dk = w_query.shape[1] // HEADS
    dv = w_value.shape[1] // HEADS
    even = [z * nx for z in range(nd // nx)]
    odd = [z * nx + 1 for z in range(nd // nx)] if nx == 2 else []
    order = even + odd
    pair = [k for k in range(ns) if not k & 1] + [k for k in range(ns) if k & 1]

    def gather_seq(own):
        got = {0: own}
        for k in range(2, ns, 2):
            got[k] = swap(own, SEQ, k)
        for k in range(1, ns, 2):
            got[k] = swap(got[k - 1], SEQ, 1)
        return got

    def scatter_seq(left, right):
        half = left.shape[0] // 2
        away = nn(left[half:], right).astype(BF16)
        got = swap(away, SEQ, 1)
        low = nn(left[:half], right) + got.astype(F32)
        total = low[:tokens]
        for at, k in enumerate(pair[1 : ns // 2], 1):
            part = low[at * tokens : (at + 1) * tokens].astype(BF16)
            got = swap(part, SEQ, k)
            if at < ns // 2 - 1:
                total = total + got.astype(F32)
        return total, got

    def row(own):
        got = gather_seq(own)
        return jnp.concatenate([got[k] for k in pair], axis=0)

    small = jnp.stack([gain_attn, gain_mlp], axis=0)
    small = jnp.concatenate([small, segments.reshape(-1, rows).astype(BF16)], axis=0)
    small = gather_seq(small)
    seg = jnp.concatenate([small[k][2:].reshape(tokens) for k in pair], axis=0)
    gains = jnp.concatenate(xor_order([small[k][:2] for k in range(ns)], j), axis=1)
    zs = [gains] + [swap(gains, DP, m) for m in even[1:]]
    zs = jnp.stack(zs, axis=0)
    parts = [zs[i] for i in range(len(even))]
    if nx == 2:
        xs = swap(zs, DP, 1)
        parts = parts + [xs[i] for i in range(len(even))]
    gains = jnp.concatenate(parts, axis=1).astype(F32)
    gain_first, gain_second = gains[0:1], gains[1:2]

    def own_block(mats):
        rel = cut_heads(mats, ns, j)
        got = [rel[0]] + [swap(rel[k], SEQ, k) for k in range(1, ns)]
        height = sum(m.shape[1] // ns for m in mats)
        return stack_rows(got, rows, [height], j)

    def own_blocks(groups, late):
        mats = [m for g in groups for m in g] + late
        heights = [sum(m.shape[1] // ns for m in g) for g in groups]
        whole = cut_heads_whole(mats, ns, j)
        if nx == 2:
            rel = pair_up(whole, swap(whole, DP, 1), j)
        else:
            rel = [whole[k] for k in range(ns)]
        got = [rel[0]] + [swap(rel[k], SEQ, k) for k in range(1, ns)]
        got = stack_rows(got, rows, heights, j, sum(m.shape[1] // ns for m in late))
        return [got[i : -1 : len(groups)] for i in range(len(groups))] + [got[-1]]

    def along(own):
        if len(even) != 4:
            return [own] + [swap(own, DP, m) for m in even[1:]]
        inner = lambda i: (i // nx) in (1, 2)
        near = swap(own, DP, nx)
        mid_a = swap_inner(own, 3 * nx, inner)
        mid_b = swap_inner(near, 3 * nx, inner)
        out_a = swap(mid_a, DP, nx)
        out_b = swap(mid_b, DP, nx)
        is_inner = ((d // nx) == 1) | ((d // nx) == 2)
        return [own, near, jnp.where(is_inner, mid_b, out_a), jnp.where(is_inner, mid_a, out_b)]

    def gather_dp(own):
        own, across = own[0], own[1:]
        blocks = along(own)
        if nx == 2:
            more = [swap(b, DP, 1) for i, b in enumerate(blocks) if i or not across]
            blocks = blocks + list(across) + more
        return jnp.concatenate(blocks, axis=1)

    def gather_dp_late(own):
        blocks = along(own)
        return jnp.concatenate([b[i] for i in range(nx) for b in blocks], axis=1)

    def reduce_line(part, stepwise):
        if stepwise and len(even) == 4:
            inner = lambda i: (i // nx) in (1, 2)

            def add(value, got):
                return (value.astype(F32) + got.astype(F32)).astype(BF16)

            third, second = part(3).astype(BF16), part(2).astype(BF16)
            in_b = swap(third, DP, nx)
            in_a = swap(second, DP, nx)
            second = add(second, in_b)
            mid_d = swap_inner(second, 3 * nx, inner)
            third = add(third, in_a)
            mid_c = swap_inner(third, 3 * nx, inner)
            is_inner = ((d // nx) == 1) | ((d // nx) == 2)
            first = add(part(1), jnp.where(is_inner, mid_d, 0))
            return [part(0), jnp.where(is_inner, mid_c, 0), swap(first, DP, nx)]
        far = range(1, len(even))
        return [part(0)] + [swap(part(i).astype(BF16), DP, even[i]) for i in far]

    def block_of(value, m):
        at = order.index(m)
        return value[:, at * wide : (at + 1) * wide]

    def scatter_dp(left, right, name):
        def part(i):
            got = 0.0
            if nx == 2:
                away = tn(left, block_of(right, even[i] + 1)).astype(BF16)
                got = swap(away, DP, 1).astype(F32)
            return tn(left, block_of(right, even[i])) + got

        return reduce_line(part, name in STEPWISE)

    def scatter_dp_late(left, right, name):
        def part(i):
            near = tn(left, block_of(right, even[i]))
            if nx == 1:
                return near[None]
            far = tn(left, block_of(right, even[i] + 1))
            return jnp.stack([near, far], axis=0)

        terms = reduce_line(part, name in STEPWISE)
        total = sum(t.astype(F32) for t in terms)
        own, away = total[0], total[nx - 1].astype(BF16)
        return [own, swap(away, DP, 1)] if nx == 2 else [own]

    def to_owners(sums):
        rel = cut_rows(sums, ns, j)
        return [rel[0]] + [swap(rel[k], SEQ, k) for k in range(1, ns)]

    qk, vw = dk * hp, dv * hp
    fw = w_up.shape[1] // ns
    out_t, down_t = w_out.T, w_down.T
    own_t = own_block([w_query, w_key, w_value, w_gate])
    own_o, own_m, own_d = own_blocks([[out_t], [w_up, w_act]], [down_t])
    w_in = gather_dp(own_t)
    w_o = gather_dp(own_o)
    wc = gather_dp(own_m)
    wd = gather_dp_late(own_d)

    x, cot, cot_half = enter(block_input, cotangent, d, order, wide)
    cot_row = row(cot_half)

    norm_one, rms_one = rms(x)
    act_one = (norm_one * gain_first).astype(BF16)
    act_one = row(act_one)
    qkv = nt(act_one, w_in)
    zgate = qkv[:, 2 * qk + vw :]

    pos = jnp.concatenate([(j ^ k) * tokens + jnp.arange(tokens, dtype=jnp.int32) for k in pair])
    diff = pos[:, None] - pos[None, :]
    allowed = (diff >= 0) & (seg[:, None] == seg[None, :])
    span = jnp.maximum(diff, 0).astype(F32)
    heads = []
    for h in range(hp):
        head = (j * hp + h).astype(F32)
        mask = jnp.where(allowed, jnp.exp(span * jnp.log1p(-jnp.exp2(-5.0 - head))), 0.0)
        q = qkv[:, h * dk : (h + 1) * dk]
        k = qkv[:, qk + h * dk : qk + (h + 1) * dk] * dk ** (-0.5)
        v = qkv[:, 2 * qk + h * dv : 2 * qk + (h + 1) * dv]
        scores = high_nt(q, k) * mask
        ret = high_nn(scores, v)
        hscale = lax.rsqrt(jnp.mean(ret * ret, axis=-1, keepdims=True) + HEAD_FLOOR)
        heads.append((mask, q, k, v, scores, ret * hscale, hscale))
    retn = jnp.concatenate([h[5] for h in heads], axis=1)
    sig = jax.nn.sigmoid(zgate)
    swish_val, swish_slope = zgate * sig, sig * (1.0 + zgate * (1.0 - sig))
    mixed = (swish_val * retn).astype(BF16)
    low, got = scatter_seq(mixed, w_o)
    resid = x + (low + got.astype(F32))

    norm_two, rms_two = rms(resid)
    act_two = (norm_two * gain_second).astype(BF16)
    act_two = row(act_two)
    both = nt(act_two, wc)
    upper, pregate = both[:, :fw], both[:, fw:]
    cdf = 0.5 * (1.0 + lax.erf(pregate * SQRT_HALF))
    dens = jnp.exp(-0.5 * pregate * pregate) * INV_ROOT_TWO_PI
    gelu_val, gelu_slope = pregate * cdf, cdf + pregate * dens
    hidden = (gelu_val * upper).astype(BF16)
    d_hidden = nt(cot_row, wd)
    d_pre = (d_hidden * upper * gelu_slope).astype(BF16)
    d_upper = (d_hidden * gelu_val).astype(BF16)
    d_both = jnp.concatenate([d_upper, d_pre], axis=1)
    low, got = scatter_seq(d_both, wc)
    sum_c = scatter_dp(d_both, act_two, "C")
    sum_d = scatter_dp_late(hidden, cot_row, "D")
    d_resid = cot + rms_backward(low + got.astype(F32), norm_two, rms_two, gain_second)

    res_half = d_resid.astype(BF16)
    res_row = row(res_half)
    late, res_row = lax.optimization_barrier((hidden, res_row))
    block_out = leave(d, order, wide, resid, *scatter_seq(late, wd))
    sum_o = scatter_dp(mixed, res_row, "O")
    d_mixed = nt(res_row, w_o)
    d_zgate = (d_mixed * retn * swish_slope).astype(BF16)
    d_retn = d_mixed * swish_val
    dqs, dks, dvs = [], [], []
    for h, (mask, q, k, v, scores, rn, hscale) in enumerate(heads):
        dr = d_retn[:, h * dv : (h + 1) * dv]
        d_ret = hscale * (dr - rn * jnp.mean(dr * rn, axis=-1, keepdims=True))
        d_scores = high_nt(d_ret, v) * mask
        dqs.append(high_nn(d_scores, k).astype(BF16))
        dks.append((high_tn(d_scores, q) * dk ** (-0.5)).astype(BF16))
        dvs.append(high_tn(scores, d_ret).astype(BF16))
    d_in = jnp.concatenate(dqs + dks + dvs + [d_zgate], axis=1)
    sum_q = scatter_dp(d_in, act_one, "Q")
    low, got = scatter_seq(d_in, w_in)
    grad_input = leave_norm(d, order, wide, d_resid, low, got, x, rms_one, gain_first)

    got = to_owners([sum_c, sum_d, sum_o])
    grad_up, grad_act, grad_down, grad_out, dots_mlp = place_heads(got, [fw, fw, fw, vw], [0, 1], [w_up, w_act], [], j)
    got = to_owners([sum_q])
    grad_query, grad_key, grad_value, grad_gate, dots_attn = place_heads(
        got, [qk, qk, vw, vw], [0, 1, 2, 3], [w_query, w_key, w_value, w_gate], [], j
    )
    grad_gain_attn = dots_attn.reshape(rows) / gain_attn.astype(F32)
    grad_gain_mlp = dots_mlp.reshape(rows) / gain_mlp.astype(F32)
    return (
        block_out,
        grad_input,
        grad_gain_attn,
        grad_query,
        grad_key,
        grad_value,
        grad_gate,
        grad_out.T,
        grad_gain_mlp,
        grad_up,
        grad_act,
        grad_down.T,
    )


STEPWISE = "CDOQ"


def solution(mesh):
    both = (DP, SEQ)
    tok, vec, down, across = P(both, None), P(both), P(both, None), P(None, both)

    return jax.shard_map(
        body,
        mesh=mesh,
        in_specs=(tok, P(DP, SEQ), tok, vec, down, down, down, down, across, vec, down, down, across),
        out_specs=(tok, tok, vec, down, down, down, down, across, vec, down, down, across),
        check_vma=False,
    )
```
